256 devices in a mesh: tm: 64 (over y, x, z_hi), row: 4 (over z_lo, core).
Axes of the slice: x: 4, y: 4, z: 8 (z_hi: 4, z_lo: 2; z = z_hi * 2 + z_lo), core: 2. Of those that a mesh axis runs over, the one named last changes fastest.
Arguments:
- latent: bfloat16 [128, 8, 40, 2240], P('tm', 'row'), may hold values from -6 to 6
- query_raw: bfloat16 [128, 8, 40, 2240], P('tm', 'row'), may hold values from -6 to 6
- key_raw: bfloat16 [128, 8, 40, 2240], P('tm', 'row'), may hold values from -12 to 12
- value_raw: bfloat16 [128, 8, 40, 2240], P('tm', 'row'), may hold values from -12 to 12
- query_gain: float32 [2240], replicated, may hold values from 0.4 to 2.5
- key_gain: float32 [2240], replicated, may hold values from 0.4 to 2.5
- space_kernel: float32 [3, 3, 2240], replicated, may hold values from -2 to 2
- time_kernel: float32 [3, 2240], replicated, may hold values from -3.5 to 3.5
- first_weight: bfloat16 [2240, 2048], P('tm', 'row'), may hold values from -0.125 to 0.125
- first_bias: float32 [2048], replicated, may hold values from -3 to 3
- second_weight: bfloat16 [2048, 1280], P('row', 'tm'), may hold values from -0.125 to 0.125
- second_bias: float32 [1280], replicated, may hold values from -3 to 3
- target_keys: bfloat16 [128, 256, 1280], P('tm', 'row'), may hold values from -410 to 410
- target_values: bfloat16 [128, 256, 1280], P('tm', 'row'), may hold values from -12 to 12
Outputs:
- blended: bfloat16 [128, 8, 40, 2240], P('tm', 'row')
- attended: bfloat16 [128, 8, 40, 1280], P('tm', 'row')
The draws below stay inside these ranges and needn't reach their ends.
All inputs are finite; a program needn't handle non-finite values.
Results may differ from the reference program's by a relative error of at most 0.01545.
The reference program's roundings to bfloat16 on the way count: a program that leaves them out, or rounds other values in their place, can miss the bound.
Values may be sent and summed in bfloat16 or wider, within the bound.
No kernel may reach another device: no remote copies, remote signals or barrier semaphores. Data moves between devices by JAX's collectives and lax.ppermute only.
A program may use at most 128 MiB of HBM per device.

```python
import math
import jax
import jax.numpy as jnp
from jax import lax

HEADS = 70
HEAD_DIM = 32
D = 2240
PROJ = 2048
AHEADS = 16
AHEAD_DIM = 80
OUTF = 1280
TGT = 256
COLS = 40
BLOCK_FRAMES = 2
FRAMES = 128
HEIGHT = 8


def paired_fields(key):
    base_key = jax.random.fold_in(key, 11)
    key_noise_key = jax.random.fold_in(base_key, 0)
    value_noise_key = jax.random.fold_in(base_key, 1)
    key_offset_key = jax.random.fold_in(base_key, 2)
    value_offset_key = jax.random.fold_in(base_key, 3)
    coef_key = jax.random.fold_in(base_key, 5)
    sign_key = jax.random.fold_in(base_key, 6)
    frame_key = jax.random.fold_in(base_key, 7)
    shape = (FRAMES, HEIGHT, COLS, D)
    key_noise = jax.random.normal(key_noise_key, shape, jnp.float32)
    value_noise = jax.random.normal(value_noise_key, shape, jnp.float32)
    spread = jnp.full((FRAMES, HEIGHT, 1, 1), 1.5, jnp.float32)
    key_offsets = spread * jax.random.normal(key_offset_key, (FRAMES, HEIGHT, 1, D), jnp.float32)
    value_offsets = spread * jax.random.normal(value_offset_key, (FRAMES, HEIGHT, 1, D), jnp.float32)
    magnitude = jax.random.uniform(coef_key, (D,), jnp.float32, 1.5, 3.0)
    signs = jnp.where(jax.random.uniform(sign_key, (D,), jnp.float32) < 0.5, -1.0, 1.0)
    frame_factor = jnp.exp(jax.random.uniform(frame_key, (FRAMES, 1, 1, 1), jnp.float32, math.log(0.6), math.log(1.6)))
    rolled = jnp.roll(key_noise.reshape(FRAMES, HEIGHT, COLS, HEADS, HEAD_DIM), 1, axis=-1).reshape(shape)
    keys_drawn = jnp.clip(key_noise + key_offsets, -12.0, 12.0).astype(jnp.bfloat16)
    values_drawn = jnp.clip(frame_factor * magnitude * signs * rolled + value_noise + value_offsets, -12.0, 12.0).astype(jnp.bfloat16)
    return (keys_drawn, values_drawn)


def draw_key_raw(key, part):
    return paired_fields(key)[0]


def draw_value_raw(key, part):
    return paired_fields(key)[1]


def draw_target_keys(key, part):
    base_key = jax.random.fold_in(jax.random.fold_in(key, 37), 0)
    shape = (FRAMES, TGT, OUTF)
    keys_drawn = jnp.clip(3.0 * jax.random.normal(base_key, shape, jnp.float32), -15.0, 15.0)
    return keys_drawn.astype(jnp.bfloat16)


def steps_of(key, extent, cuts, smallest, largest):
    def one(axis_at, shards_of):
        draws = jax.random.uniform(jax.random.fold_in(jax.random.fold_in(key, 6), axis_at), (shards_of,), jnp.float32, smallest / len(cuts), largest / len(cuts))
        return jnp.repeat(jnp.exp(draws), extent[axis_at] // shards_of).reshape((-1,) + (1,) * (len(extent) - axis_at - 1))

    gain = one(*cuts[0])
    for cut in cuts[1:]:
        gain = gain * one(*cut)
    return gain


def bell_draw(stream_key, extent, scale, reach, cuts=(), held_as=jnp.bfloat16):
    values = scale * jax.random.normal(stream_key, extent, jnp.float32)
    if cuts:
        values = values * steps_of(stream_key, extent, cuts, -0.22, 0.18)
    return jnp.clip(values, -reach, reach).astype(held_as)


def setup_inputs(seed: int = 0) -> dict:
    streams_of = jax.random.split(jax.random.key(seed), 15)
    latent = bell_draw(streams_of[0], (FRAMES, HEIGHT, COLS, D), 1.0, 6.0, ((0, 64), (1, 4)))
    query_raw = bell_draw(streams_of[1], (FRAMES, HEIGHT, COLS, D), 1.0, 6.0, ((0, 64), (1, 4)))
    key_raw = draw_key_raw(jax.random.fold_in(streams_of[14], 71), 0)
    value_raw = draw_value_raw(jax.random.fold_in(streams_of[14], 71), 0)
    query_gain = jnp.clip(jnp.exp(jax.random.uniform(streams_of[4], (D,), jnp.float32, math.log(0.4), math.log(2.5))), 0.4, 2.5)
    key_gain = jnp.clip(jnp.exp(jax.random.uniform(streams_of[5], (D,), jnp.float32, math.log(0.4), math.log(2.5))), 0.4, 2.5)
    space_kernel = bell_draw(streams_of[6], (3, 3, D), 9 ** -0.5, 2.0, (), jnp.float32)
    time_kernel = bell_draw(streams_of[7], (3, D), 3 ** -0.5, 3.5, (), jnp.float32)
    first_weight = bell_draw(streams_of[8], (D, PROJ), D ** -0.5, 0.125, ((0, 64), (1, 4)))
    first_bias = bell_draw(streams_of[9], (PROJ,), 0.5, 3.0, (), jnp.float32)
    second_weight = bell_draw(streams_of[10], (PROJ, OUTF), PROJ ** -0.5, 0.125, ((0, 4), (1, 64)))
    second_bias = bell_draw(streams_of[11], (OUTF,), 0.5, 3.0, (), jnp.float32)
    target_keys = draw_target_keys(jax.random.fold_in(streams_of[14], 71), 0)
    target_values = bell_draw(streams_of[13], (FRAMES, TGT, OUTF), 2.0, 12.0, ((0, 64), (1, 4)))
    return {"latent": latent, "query_raw": query_raw, "key_raw": key_raw, "value_raw": value_raw, "query_gain": query_gain, "key_gain": key_gain, "space_kernel": space_kernel, "time_kernel": time_kernel, "first_weight": first_weight, "first_bias": first_bias, "second_weight": second_weight, "second_bias": second_bias, "target_keys": target_keys, "target_values": target_values}


def head_features(source, scaling):
    values = source.astype(jnp.float32).reshape(source.shape[:-1] + (HEADS, HEAD_DIM))
    mean_square = jnp.maximum(lax.optimization_barrier(jnp.mean(values * values, axis=-1, keepdims=True)), 0.25)
    return jax.nn.relu(values * lax.rsqrt(mean_square) * scaling.reshape(HEADS, HEAD_DIM))

def frame_softmax(query_split, key_split, value_split):
    score_scale = 1.0 / AHEAD_DIM ** 0.5
    scores = jnp.einsum('cqgd,ckgd->cgqk', query_split.astype(jnp.float32), key_split.astype(jnp.float32), precision=lax.Precision.HIGHEST) * score_scale
    row_max = lax.optimization_barrier(jnp.max(scores, axis=-1, keepdims=True))
    weights = jnp.exp(scores - row_max)
    row_total = lax.optimization_barrier(jnp.sum(weights, axis=-1))
    weights_low = lax.optimization_barrier(weights.astype(jnp.bfloat16))
    result = jnp.einsum('cgqk,ckgd->cqgd', weights_low.astype(jnp.float32), value_split.astype(jnp.float32), precision=lax.Precision.HIGHEST)
    return result / jnp.transpose(row_total, (0, 2, 1))[..., None]

def reference(latent, query_raw, key_raw, value_raw, query_gain, key_gain, space_kernel, time_kernel, first_weight, first_bias, second_weight, second_bias, target_keys, target_values):
    block_count = FRAMES // BLOCK_FRAMES

    def shaped(source):
        return source.reshape((block_count, BLOCK_FRAMES) + source.shape[1:])

    def block_sums(inputs):
        key_part, value_part = inputs
        key_feat = head_features(key_part, key_gain)
        value_feat = value_part.astype(jnp.float32).reshape(key_feat.shape)
        key_state = jnp.einsum('crwhd,crwhe->dhe', key_feat, value_feat, precision=lax.Precision.HIGHEST).reshape(HEAD_DIM, D)
        return (key_state, lax.optimization_barrier(jnp.sum(key_feat, axis=(0, 1, 2))).reshape(D))
    states, keysums = lax.map(block_sums, (shaped(key_raw), shaped(value_raw)))
    states = jnp.cumsum(states, axis=0)
    keysums = jnp.cumsum(keysums, axis=0)

    def attend(inputs):
        query_part, residue, key_state, key_total = inputs
        query_feat = head_features(query_part, query_gain)
        numerator = jnp.einsum('crwhd,dhe->crwhe', query_feat, key_state.reshape(HEAD_DIM, HEADS, HEAD_DIM), precision=lax.Precision.HIGHEST)
        denominator = jnp.einsum('crwhd,hd->crwh', query_feat, key_total.reshape(HEADS, HEAD_DIM), precision=lax.Precision.HIGHEST) + 1e-06
        linear_out = (numerator / denominator[..., None]).reshape(residue.shape)
        return (residue.astype(jnp.float32) + linear_out).astype(jnp.bfloat16)
    hidden_in = lax.map(attend, (shaped(query_raw), shaped(latent), states, keysums)).reshape(latent.shape)
    padded = jnp.pad(hidden_in, ((1, 1), (1, 1), (1, 1), (0, 0)))

    def finish(inputs):
        position, key_part, value_part = inputs
        first_frame = (position * BLOCK_FRAMES).astype(jnp.int32)
        anchor = jnp.zeros((), jnp.int32)
        window = lax.dynamic_slice(padded, (first_frame, anchor, anchor, anchor), (BLOCK_FRAMES + 2, HEIGHT + 2, COLS + 2, D))
        center = window[1:-1, 1:-1, 1:-1].astype(jnp.float32)
        spatial = jnp.zeros(center.shape, jnp.float32)
        for shift_row in range(3):
            for shift_col in range(3):
                spatial = spatial + space_kernel[shift_row, shift_col] * window[1:-1, shift_row:shift_row + HEIGHT, shift_col:shift_col + COLS].astype(jnp.float32)
        temporal = jnp.zeros(center.shape, jnp.float32)
        for shift_time in range(3):
            temporal = temporal + time_kernel[shift_time] * window[shift_time:shift_time + BLOCK_FRAMES, 1:-1, 1:-1].astype(jnp.float32)
        blended = (center + spatial + temporal).astype(jnp.bfloat16)
        tokens = blended.reshape(-1, D)
        hidden_units = jax.nn.silu(jnp.dot(tokens, first_weight, preferred_element_type=jnp.float32) + first_bias).astype(jnp.bfloat16)
        queries = (jnp.dot(hidden_units, second_weight, preferred_element_type=jnp.float32) + second_bias).astype(jnp.bfloat16)
        query_split = queries.reshape(BLOCK_FRAMES, HEIGHT * COLS, AHEADS, AHEAD_DIM)
        key_split = key_part.reshape(BLOCK_FRAMES, TGT, AHEADS, AHEAD_DIM)
        value_split = value_part.reshape(BLOCK_FRAMES, TGT, AHEADS, AHEAD_DIM)
        result = frame_softmax(query_split, key_split, value_split)
        return (blended, result.reshape(BLOCK_FRAMES, HEIGHT, COLS, OUTF).astype(jnp.bfloat16))
    blended, attended = lax.map(finish, (jnp.arange(block_count), shaped(target_keys), shaped(target_values)))
    return (blended.reshape(latent.shape), attended.reshape(FRAMES, HEIGHT, COLS, OUTF))
```

```python
import jax
import jax.numpy as jnp
from jax import lax
from jax.experimental import pallas as pl
from jax.experimental.pallas import tpu as pltpu
from jax.sharding import PartitionSpec as P

HEADS = 70
HEAD_DIM = 32
AHEADS = 16
AHEAD_DIM = 80
D = 2240
GROUPS = 18
LANES = 384
STEPS = 6
PER_STEP = LANES // 128
TOKENS = 160
STATE_ROWS = 608
KEY_ROW = GROUPS * HEAD_DIM
LINE_K = 140
LINE_PAD = 144
PADDED = 16 * LINE_PAD
PROJ = 2048
OUTF = 1280
FRAME_TOKENS = 80
BOTH = ("tm", "row")
F32 = jnp.float32
BF16 = jnp.bfloat16


def block_ones():
    rows = lax.broadcasted_iota(jnp.int32, (128, 128), 0) // HEAD_DIM
    cols = lax.broadcasted_iota(jnp.int32, (128, 128), 1) // HEAD_DIM
    return rows == cols


def split(value):
    high = value.astype(BF16)
    return high, (value - high.astype(F32)).astype(BF16)


def dot(left, right, dims=((1,), (0,))):
    return lax.dot_general(left, right, (dims, ((), ())), preferred_element_type=F32)


def features(raw, gain, ones):
    square_high, square_low = split(raw * raw)
    mean = (dot(square_high, ones) + dot(square_low, ones)) * (1.0 / HEAD_DIM)
    return jnp.maximum(raw * lax.rsqrt(jnp.maximum(mean, 0.25)) * gain, 0.0)


def lane_mask(step, j, rows):
    lane = lax.broadcasted_iota(jnp.int32, (rows, 128), 1)
    return lane + (step * LANES + j * 128) < D


def state_kernel(key_ref, value_ref, gain_ref, out_ref):
    step = pl.program_id(0)

    @pl.when(step == 0)
    def _():
        out_ref[KEY_ROW:STATE_ROWS, :] = jnp.zeros((STATE_ROWS - KEY_ROW, 128), F32)

    same = block_ones()
    ones = jnp.where(same, 1.0, 0.0).astype(BF16)
    for j in range(PER_STEP):
        lanes = slice(j * 128, (j + 1) * 128)
        mask = lane_mask(step, j, TOKENS)
        raw = jnp.where(mask, key_ref[:, lanes].astype(F32), 0.0)
        value = jnp.where(mask, value_ref[:, lanes].astype(F32), 0.0).astype(BF16)
        gain = jnp.where(lane_mask(step, j, 1), gain_ref[:, lanes], 0.0)
        feat = features(raw, gain, ones)
        high, low = split(feat)
        product = dot(high, value, ((0,), (0,))) + dot(low, value, ((0,), (0,)))
        product = jnp.where(same, product, 0.0)
        compact = product[0:32] + product[32:64] + product[64:96] + product[96:128]
        group = step * PER_STEP + j
        out_ref[pl.ds(pl.multiple_of(group * HEAD_DIM, HEAD_DIM), HEAD_DIM), :] = compact
        out_ref[pl.ds(KEY_ROW + group, 1), :] = jnp.sum(feat, axis=0, keepdims=True)


def local_state(key_raw, value_raw, key_gain):
    return pl.pallas_call(
        state_kernel,
        grid=(STEPS,),
        in_specs=[
            pl.BlockSpec((TOKENS, LANES), lambda i: (0, i)),
            pl.BlockSpec((TOKENS, LANES), lambda i: (0, i)),
            pl.BlockSpec((1, LANES), lambda i: (0, i)),
        ],
        out_specs=pl.BlockSpec((STATE_ROWS, 128), lambda i: (0, 0)),
        out_shape=jax.ShapeDtypeStruct((STATE_ROWS, 128), F32),
        name="local_state",
    )(key_raw, value_raw, key_gain)


def apply_kernel(query_ref, latent_ref, gain_ref, state_ref, out_ref):
    step = pl.program_id(0)
    same = block_ones()
    ones = jnp.where(same, 1.0, 0.0).astype(BF16)
    for j in range(PER_STEP):
        lanes = slice(j * 128, (j + 1) * 128)
        raw = jnp.where(lane_mask(step, j, TOKENS), query_ref[:, lanes].astype(F32), 0.0)
        gain = jnp.where(lane_mask(step, j, 1), gain_ref[:, lanes], 0.0)
        feat = features(raw, gain, ones)
        group = step * PER_STEP + j
        compact = state_ref[pl.ds(pl.multiple_of(group * HEAD_DIM, HEAD_DIM), HEAD_DIM), :]
        keys = state_ref[pl.ds(KEY_ROW + group, 1), :]
        wide = jnp.where(same, jnp.concatenate([compact] * 4, axis=0), 0.0)
        wide_high, wide_low = split(wide)
        high, low = split(feat)
        numerator = dot(high, wide_high) + dot(low, wide_high) + dot(high, wide_low)
        scaled_high, scaled_low = split(feat * keys)
        denominator = dot(scaled_high, ones) + dot(scaled_low, ones) + 1e-06
        out_ref[:, lanes] = (latent_ref[:, lanes].astype(F32) + numerator / denominator).astype(
            BF16
        )


def apply_state(query_raw, latent, query_gain, state):
    return pl.pallas_call(
        apply_kernel,
        grid=(STEPS,),
        in_specs=[
            pl.BlockSpec((TOKENS, LANES), lambda i: (0, i)),
            pl.BlockSpec((TOKENS, LANES), lambda i: (0, i)),
            pl.BlockSpec((1, LANES), lambda i: (0, i)),
            pl.BlockSpec((STATE_ROWS, 128), lambda i: (0, 0)),
        ],
        out_specs=pl.BlockSpec((TOKENS, LANES), lambda i: (0, i)),
        out_shape=jax.ShapeDtypeStruct((TOKENS, D), BF16),
        name="apply_state",
    )(query_raw, latent, query_gain, state)


def mix_kernel(
    own_ref, before_ref, after_ref, above_ref, below_ref, space_ref, time_ref, out_ref, pad_ref, last_ref
):
    step = pl.program_id(0)
    column = lax.broadcasted_iota(jnp.int32, (40, 128), 0)
    for j in range(PER_STEP):
        lanes = slice(j * 128, (j + 1) * 128)
        space = [[space_ref[3 * a + b : 3 * a + b + 1, lanes] for b in range(3)] for a in range(3)]
        time = [time_ref[a : a + 1, lanes] for a in range(3)]
        middle = 1.0 + space[1][1] + time[1]
        own = [[own_ref[f, r, :, lanes].astype(F32) for r in range(2)] for f in range(2)]
        before = [before_ref[r, :, lanes].astype(F32) for r in range(2)]
        after = [after_ref[r, :, lanes].astype(F32) for r in range(2)]
        above = [above_ref[f, :, lanes].astype(F32) for f in range(2)]
        below = [below_ref[f, :, lanes].astype(F32) for f in range(2)]
        tiles = []
        for f in range(2):
            for r in range(2):
                up = above[f] if r == 0 else own[f][0]
                down = below[f] if r == 1 else own[f][1]
                here = own[f][r]
                past = before[r] if f == 0 else own[0][r]
                future = after[r] if f == 1 else own[1][r]
                left = space[0][0] * up + space[1][0] * here + space[2][0] * down
                right = space[0][2] * up + space[1][2] * here + space[2][2] * down
                total = middle * here + space[0][1] * up + space[2][1] * down
                total = total + time[0] * past + time[2] * future
                total = total + jnp.where(column == 0, 0.0, pltpu.roll(left, 1, 0))
                total = total + jnp.where(column == 39, 0.0, pltpu.roll(right, 39, 0))
                tile = total.astype(BF16)
                out_ref[f, r, :, lanes] = tile
                tiles.append(total)
        whole = jnp.concatenate(tiles, axis=0)
        whole = jnp.where(lane_mask(step, j, TOKENS), whole, 0.0).astype(BF16)
        previous = last_ref[...]
        if j == 0:
            previous = jnp.where(step == 0, jnp.zeros_like(previous), previous)
        start = step * LANES + j * 128
        target = lax.broadcasted_iota(jnp.int32, (128, 128), 1) + start
        line = (target * 3641) >> 19
        inside = target - line * LINE_PAD
        source = line * LINE_K + inside - start
        row = lax.broadcasted_iota(jnp.int32, (128, 128), 0)
        valid = inside < LINE_K
        here_pick = jnp.where((source == row) & valid, 1.0, 0.0).astype(BF16)
        past_pick = jnp.where((source + 128 == row) & valid, 1.0, 0.0).astype(BF16)
        pad_ref[:, lanes] = (dot(whole, here_pick) + dot(previous, past_pick)).astype(BF16)
        last_ref[...] = whole


def mix(own, before, after, above, below, space_kernel, time_kernel):
    halo = pl.BlockSpec((2, 40, LANES), lambda i: (0, 0, i))
    return pl.pallas_call(
        mix_kernel,
        grid=(STEPS,),
        in_specs=[
            pl.BlockSpec((2, 2, 40, LANES), lambda i: (0, 0, 0, i)),
            halo,
            halo,
            halo,
            halo,
            pl.BlockSpec((9, LANES), lambda i: (0, i)),
            pl.BlockSpec((3, LANES), lambda i: (0, i)),
        ],
        out_specs=[
            pl.BlockSpec((2, 2, 40, LANES), lambda i: (0, 0, 0, i)),
            pl.BlockSpec((TOKENS, LANES), lambda i: (0, i)),
        ],
        out_shape=[
            jax.ShapeDtypeStruct((2, 2, 40, D), BF16),
            jax.ShapeDtypeStruct((TOKENS, PADDED), BF16),
        ],
        scratch_shapes=[pltpu.VMEM((TOKENS, 128), BF16)],
        name="mix",
    )(own, before, after, above, below, space_kernel, time_kernel)


CHUNK = 512
CHUNKS = PROJ // CHUNK


def project_kernel(
    token_ref,
    first_bias_ref,
    second_bias_ref,
    key_ref,
    value_ref,
    weight_ref,
    out_ref,
    first_ref,
    second_ref,
    hidden_ref,
    query_ref,
    first_sem,
    second_sem,
):
    def first_copy(n):
        return pltpu.make_async_copy(
            weight_ref.at[:, pl.ds(0, LINE_PAD), pl.ds(n * CHUNK, CHUNK)],
            first_ref.at[n],
            first_sem.at[n],
        )

    second_copy = pltpu.make_async_copy(
        weight_ref.at[:, pl.ds(LINE_PAD, AHEAD_DIM), :], second_ref, second_sem
    )
    for n in range(CHUNKS):
        first_copy(n).start()
    second_copy.start()
    for n in range(CHUNKS):
        first_copy(n).wait()
        columns = slice(n * CHUNK, (n + 1) * CHUNK)
        part = dot(token_ref[...], first_ref[n].reshape(PADDED, CHUNK)) + first_bias_ref[:, columns]
        hidden_ref[:, columns] = (part * jax.nn.sigmoid(part)).astype(BF16)
    second_copy.wait()
    query_ref[...] = (
        dot(hidden_ref[...], second_ref[...].reshape(OUTF, PROJ), ((1,), (1,))) + second_bias_ref[...]
    ).astype(BF16)
    scale = 1.0 / AHEAD_DIM**0.5
    lane = lax.broadcasted_iota(jnp.int32, (FRAME_TOKENS, 256), 1)
    for f in range(2):
        rows = slice(f * FRAME_TOKENS, (f + 1) * FRAME_TOKENS)
        tiles = [jnp.zeros((FRAME_TOKENS, 128), F32) for _ in range(OUTF // 128)]
        for head in range(AHEADS):
            tile = min(head * AHEAD_DIM // 128, OUTF // 128 - 2)
            begin = head * AHEAD_DIM - tile * 128
            window = slice(tile * 128, tile * 128 + 256)
            mine = (lane >= begin) & (lane < begin + AHEAD_DIM)
            query = query_ref[rows, window]
            query = jnp.where(mine, query, jnp.zeros_like(query))
            scores = dot(query, key_ref[f, :, window], ((1,), (1,))) * scale
            weights = jnp.exp(scores - jnp.max(scores, axis=1, keepdims=True))
            totals = jnp.sum(weights, axis=1, keepdims=True)
            result = dot(weights.astype(BF16), value_ref[f, :, window]) / totals
            result = jnp.where(mine, result, 0.0)
            tiles[tile] = tiles[tile] + result[:, :128]
            tiles[tile + 1] = tiles[tile + 1] + result[:, 128:]
        for index, tile in enumerate(tiles):
            out_ref[rows, index * 128 : (index + 1) * 128] = tile.astype(BF16)


def project_attend(tokens, first_bias, second_bias, keys, values, weights):
    vmem = pl.BlockSpec(memory_space=pltpu.VMEM)
    return pl.pallas_call(
        project_kernel,
        in_specs=[vmem] * 5 + [pl.BlockSpec(memory_space=pl.ANY)],
        out_specs=vmem,
        out_shape=jax.ShapeDtypeStruct((TOKENS, OUTF), BF16),
        scratch_shapes=[
            pltpu.VMEM((CHUNKS, 16, LINE_PAD, CHUNK), BF16),
            pltpu.VMEM((16, AHEAD_DIM, PROJ), BF16),
            pltpu.VMEM((TOKENS, PROJ), BF16),
            pltpu.VMEM((TOKENS, OUTF), BF16),
            pltpu.SemaphoreType.DMA((CHUNKS,)),
            pltpu.SemaphoreType.DMA,
        ],
        name="project_attend",
    )(tokens, first_bias, second_bias, keys, values, weights)


def line_groups():
    return [[line * 16 + i for i in range(16)] for line in range(16)]


def plane_groups():
    return [[line * 16 + i for line in range(16)] for i in range(16)]


def shifted(value, stride, distance):
    pairs = []
    for t in range(64):
        digit = (t // stride) % 4
        pairs.append((t, t + ((digit + distance) % 4 - digit) * stride))
    return lax.ppermute(value, "tm", pairs)


def ring_prefix(value, stride):
    digit = (lax.axis_index("tm") // stride) % 4
    moved = [shifted(value, stride, distance) for distance in (1, 2, 3)]
    earlier = sum(jnp.where(digit >= d + 1, part, 0.0) for d, part in enumerate(moved))
    return earlier, value + moved[0] + moved[1] + moved[2]


def state_prefix(local):
    pieces = lax.all_to_all(local, "row", 0, 0, tiled=True)
    block = jnp.sum(pieces.reshape(4, STATE_ROWS // 4, 128), axis=0)
    along_z, total = ring_prefix(block, 1)
    along_x, total = ring_prefix(total, 4)
    along_y, _ = ring_prefix(total, 16)
    return lax.all_gather(block + along_z + along_x + along_y, "row", axis=0, tiled=True)


def line_weights(first_weight, second_weight):
    shard = jnp.concatenate([first_weight, second_weight.T], axis=0)
    line = lax.all_gather(shard, BOTH, axis=0, axis_index_groups=line_groups())
    line = line.reshape(4, 4, 55, 512)
    first = jnp.transpose(line[:, :, :35], (0, 2, 1, 3)).reshape(LINE_K, PROJ)
    first = jnp.pad(first, ((0, LINE_PAD - LINE_K), (0, 0)))
    second = jnp.transpose(line[:, :, 35:], (0, 2, 1, 3)).reshape(AHEAD_DIM, PROJ)
    return jnp.concatenate([first, second], axis=0)


def per_device(
    latent,
    query_raw,
    key_raw,
    value_raw,
    query_gain,
    key_gain,
    space_kernel,
    time_kernel,
    first_weight,
    first_bias,
    second_weight,
    second_bias,
    target_keys,
    target_values,
):
    line = line_weights(first_weight, second_weight)
    weights = lax.all_gather(line, BOTH, axis=0, axis_index_groups=plane_groups())
    key_raw, _ = lax.optimization_barrier((key_raw, line))

    across = [(i, i ^ 2) for i in range(4)]
    beside = [(i, i ^ 1) for i in range(4)]
    targets = []
    for mine in (target_keys, target_values):
        other = lax.ppermute(mine, "row", across)
        chip = jnp.concatenate([mine, other], axis=1)
        partner = lax.ppermute(chip, "row", beside)
        targets.append(jnp.concatenate([chip, partner], axis=1))

    local = local_state(
        key_raw.reshape(TOKENS, D), value_raw.reshape(TOKENS, D), key_gain.reshape(1, D)
    )
    state = state_prefix(local)
    hidden = apply_state(
        query_raw.reshape(TOKENS, D), latent.reshape(TOKENS, D), query_gain.reshape(1, D), state
    ).reshape(2, 2, 40, D)
    count = lax.axis_size("tm")
    forward = [(i, i + 1) for i in range(count - 1)]
    backward = [(i + 1, i) for i in range(count - 1)]
    before = lax.ppermute(hidden[1], "tm", forward)
    after = lax.ppermute(hidden[0], "tm", backward)
    down = [(i, i + 1) for i in range(3)]
    up = [(i + 1, i) for i in range(3)]
    above = lax.ppermute(hidden[:, 1], "row", down)
    below = lax.ppermute(hidden[:, 0], "row", up)
    blended, tokens = mix(
        hidden, before, after, above, below, space_kernel.reshape(9, D), time_kernel
    )
    attended = project_attend(
        tokens,
        first_bias.reshape(1, PROJ),
        second_bias.reshape(1, OUTF),
        targets[0],
        targets[1],
        weights,
    )
    return (blended, attended.reshape(2, 2, 40, OUTF))


def solution(mesh):
    return jax.shard_map(
        per_device,
        mesh=mesh,
        in_specs=(
            P("tm", "row", None, None),
            P("tm", "row", None, None),
            P("tm", "row", None, None),
            P("tm", "row", None, None),
            P(),
            P(),
            P(),
            P(),
            P("tm", "row"),
            P(),
            P("row", "tm"),
            P(),
            P("tm", "row", None),
            P("tm", "row", None),
        ),
        out_specs=(P("tm", "row", None, None), P("tm", "row", None, None)),
        check_vma=False,
    )
```
